32 devices in a mesh: regions: 2 (over y), gz: 8 (over z, x), gy: 2 (over core).
Axes of the slice: x: 2, y: 2, z: 4, core: 2. Of those that a mesh axis runs over, the one named last changes fastest.
Arguments:
- iterate: float32 [16, 32, 128, 256], P(None, ('regions', 'gz'), 'gy'), parts along dimension 1, may hold values from -6 to 6
- residual: float32 [16, 32, 128, 256], P(None, ('regions', 'gz'), 'gy'), parts along dimension 1, may hold values from -16 to 16
- labels: int32 [32, 128, 256], P(('regions', 'gz'), 'gy'), parts along dimension 0, may hold values from 0 to 7
- boundary: int32 [32, 128, 256], P(('regions', 'gz'), 'gy'), parts along dimension 0, may hold values 0 or 1
Outputs:
- iterate_out: float32 [16, 32, 128, 256], P(None, ('regions', 'gz'), 'gy'), parts along dimension 1
- residual_out: float32 [16, 32, 128, 256], P(None, ('regions', 'gz'), 'gy'), parts along dimension 1
The draws below stay inside these ranges and needn't reach their ends.
There are 2 independent parts, one for each index of `regions`. The reference program is written for one: setup_inputs(seed, part) draws one part's arguments, and reference() takes and returns one part's arrays. A program takes and returns all parts, laid end to end along the dimension named above; each array names one. Nothing has to cross between parts.
All inputs are finite; a program needn't handle non-finite values. No bound on the sum of `boundary` on one device may be relied on, other than what follows from the above.
Results may differ from the reference program's by a relative error of at most 0.0003.
Values sent between devices are 32-bit elements; how exact they have to be, the bound alone decides.
A program may use at most 128 MiB of HBM per device.

```python
import math
import jax
import jax.numpy as jnp
from jax import lax

RHS = 16
NCLASS = 8
ITERS = 3
NX = 256
NZ = 16
NY = 128


def draw_residual(key, part):
    base_key = jax.random.fold_in(key, 7)
    scale_key, random_key = jax.random.split(base_key, 2)
    column_scale = jnp.exp(jax.random.uniform(scale_key, (RHS,), jnp.float32, math.log(0.3), math.log(3.0)))
    depth_pos = jnp.arange(NZ, dtype=jnp.float32) / max(NZ - 1, 1)
    depth_scale = jnp.exp((depth_pos - 0.5) * math.log(3.0))
    random_part = jax.random.normal(random_key, (RHS, NZ, NY, NX), jnp.float32)
    values = column_scale[:, None, None, None] * depth_scale[None, :, None, None] * random_part
    return jnp.clip(values, -16.0, 16.0)


def touch_ends(array, own_key, smallest, high):
    shape = array.shape
    index_at = [jax.random.randint(jax.random.fold_in(own_key, axis), (), 0, shape[axis]) for axis in range(len(shape))]
    array = array.at[tuple(index_at)].set(smallest)
    longest = shape.index(max(shape))
    index_at[longest] = (index_at[longest] + 1) % shape[longest]
    return array.at[tuple(index_at)].set(high)


def levels(own_key, dims, cuts, least, largest):
    def one(dim, parts):
        draws = jax.random.uniform(jax.random.fold_in(jax.random.fold_in(own_key, 6), dim), (parts,), jnp.float32, least / len(cuts), largest / len(cuts))
        return jnp.repeat(jnp.exp(draws), dims[dim] // parts).reshape((-1,) + (1,) * (len(dims) - dim - 1))

    level = one(*cuts[0])
    for cut in cuts[1:]:
        level = level * one(*cut)
    return level


def gaussian(own_key, extent, deviation, reach, cuts=(), held_as=jnp.bfloat16):
    factor_of = levels(own_key, extent, cuts, -0.22, 0.18) if cuts else 1.0
    drawn = jax.random.normal(own_key, extent, jnp.float32) * deviation * factor_of
    return jnp.minimum(jnp.maximum(drawn, -reach), reach).astype(held_as)


def setup_inputs(seed: int = 0, part: int = 0) -> dict:
    key_of = jax.random.split(jax.random.key(seed), 5)
    own_keys = jax.random.split(jax.random.fold_in(key_of[4], part), 5)
    iterate = gaussian(own_keys[0], (RHS, NZ, NY, NX), 1.0, 6.0, ((1, 8), (2, 2)), jnp.float32)
    residual = draw_residual(jax.random.fold_in(jax.random.fold_in(key_of[4], part), 71), part)
    labels = touch_ends(jax.random.randint(own_keys[2], (NZ, NY, NX), 0, NCLASS), jax.random.fold_in(own_keys[2], 1), 0, NCLASS - 1).astype(jnp.int32)
    boundary = touch_ends((jax.random.randint(own_keys[3], (NZ, NY, NX), 0, 8) < 1).astype(jnp.int32), jax.random.fold_in(own_keys[3], 1), 0, 1)
    return {"iterate": iterate, "residual": residual, "labels": labels, "boundary": boundary}


contrast_log = 4.0 * math.log(10.0)
highest = lax.Precision.HIGHEST

def shift_cells(block, forward):
    widths = [(0, 0)] * (block.ndim - 1)
    if forward:
        return jnp.pad(block[..., 1:], widths + [(0, 1)])
    return jnp.pad(block[..., :-1], widths + [(1, 0)])

def neighbors(extended):
    center = extended[..., 1:-1, 1:-1, :]
    beside = [extended[..., 2:, 1:-1, :], extended[..., :-2, 1:-1, :], extended[..., 1:-1, 2:, :], extended[..., 1:-1, :-2, :], shift_cells(center, True), shift_cells(center, False)]
    return (center, beside)

def couplings_of(extended):
    coef_center, coef_beside = neighbors(extended[0])
    inner_center, inner_beside = neighbors(extended[1])
    diagonal = jnp.zeros_like(coef_center)
    offsets = []
    for neighbor_coef, neighbor_inner in zip(coef_beside, inner_beside):
        face_coef = jnp.where(neighbor_coef > 0.0, 2.0 * coef_center * neighbor_coef / (coef_center + neighbor_coef), coef_center)
        diagonal = diagonal + face_coef
        offsets.append(inner_center * face_coef * neighbor_inner)
    diagonal = inner_center * diagonal + (1.0 - inner_center)
    return (diagonal, offsets)

def apply_operator(diagonal, offsets, extended):
    center, beside = neighbors(extended)
    coupled = offsets[0] * beside[0]
    for weight, values in zip(offsets[1:], beside[1:]):
        coupled = coupled + weight * values
    return diagonal * center - coupled

def cell_fields(labels, boundary):
    coef = jnp.exp(labels.astype(jnp.float32) * (contrast_log / (NCLASS - 1)))
    interior = (1 - boundary).astype(jnp.float32)
    return jnp.stack([coef, interior])

def gram(left_block, right_block):
    left_flat = left_block.reshape(left_block.shape[0], -1)
    right_flat = right_block.reshape(right_block.shape[0], -1)
    return lax.dot_general(left_flat, right_flat, (((1,), (1,)), ((), ())), precision=highest)

def combine(block, weights):
    flat = block.reshape(block.shape[0], -1)
    mixed = lax.dot_general(weights, flat, (((0,), (0,)), ((), ())), precision=highest)
    return mixed.reshape(block.shape)

def spd_solve(matrix, right):
    factor = jnp.linalg.cholesky(matrix)
    return jax.scipy.linalg.cho_solve((factor, True), right)

def reference(iterate, residual, labels, boundary):
    fields = cell_fields(labels, boundary)
    extended = jnp.pad(fields, ((0, 0), (1, 1), (1, 1), (0, 0)))
    diagonal, offsets = couplings_of(extended)
    inverse_diag = 1.0 / diagonal
    scaled = inverse_diag * residual
    direction = scaled
    summed_rho = gram(residual, scaled)
    for iteration in range(ITERS):
        direction_ext = jnp.pad(direction, ((0, 0), (1, 1), (1, 1), (0, 0)))
        image = apply_operator(diagonal, offsets, direction_ext)
        curvature = gram(direction, image)
        step_size = spd_solve(curvature, summed_rho)
        iterate = iterate + combine(direction, step_size)
        residual = residual - combine(image, step_size)
        if iteration + 1 < ITERS:
            scaled = inverse_diag * residual
            next_rho = gram(residual, scaled)
            momentum = spd_solve(summed_rho, next_rho)
            direction = scaled + combine(direction, momentum)
            summed_rho = next_rho
    return (iterate, residual)
```

```python
import functools
import math

import jax
import jax.numpy as jnp
from jax import lax
from jax.experimental import pallas as pl
from jax.experimental.pallas import tpu as pltpu
from jax.sharding import PartitionSpec as P

NCLASS = 8
ITERS = 3
DEPTH = ITERS
YH = 4
OFF = YH + 1
LH = 8
SHIFT = LH - OFF
GROUP = 4
REDUCES = 2 * ITERS - 1

contrast_log = 4.0 * math.log(10.0)
MESH = pl.DeviceIdType.MESH
F32 = jnp.float32
BF16 = jnp.bfloat16


def split(value):
    high = value.astype(BF16)
    return high, (value - high.astype(F32)).astype(BF16)


def dot_nt(left, right):
    return lax.dot_general(left, right, (((1,), (1,)), ((), ())), preferred_element_type=F32)


def exact(left, right, contract):
    parts = []
    for value in (left, right):
        first, rest = split(value)
        third = (value - first.astype(F32) - rest.astype(F32)).astype(BF16)
        parts.append((first, rest, third))
    result = None
    for i, j in ((2, 0), (1, 1), (0, 2), (1, 0), (0, 1), (0, 0)):
        term = lax.dot_general(parts[0][i], parts[1][j], (contract, ((), ())), preferred_element_type=F32)
        result = term if result is None else result + term
    return result


def exact_nt(left, right):
    return exact(left, right, ((1,), (1,)))


def exact_nn(left, right):
    return exact(left, right, ((1,), (0,)))


def eliminate(matrix):
    m = matrix.shape[0]
    row_id = lax.broadcasted_iota(jnp.int32, matrix.shape, 0)
    for k in range(m):
        pivot_row = matrix[k : k + 1, :] / matrix[k : k + 1, k : k + 1]
        matrix = jnp.where(row_id == k, pivot_row, matrix - matrix[:, k : k + 1] * pivot_row)
    return matrix


def kernel(
    sizes,
    iterate, residual, labels, boundary, iterate_out, residual_out,
    X, R, D, IM, LAB, BND, COEF, INNER, INV, DIAG, WZU, WZD, WYU, WYD, WXR, WXL,
    acc, gsend, gslots, wbuf,
    local_sem, bulk_send, bulk_recv, strip_send, strip_recv, gram_send, gram_recv, out_sem,
):
    gz_count, gy_count, m, nz, ny, nx = sizes
    total = gz_count * gy_count
    region = lax.axis_index("regions")
    gz = lax.axis_index("gz")
    gy = lax.axis_index("gy")
    me = gz * gy_count + gy
    rows_window = ny + YH if gy_count == 2 else ny + 2 * YH
    start = OFF - YH * jnp.minimum(gy, 1) if gy_count == 2 else OFF - YH

    barrier = pltpu.get_barrier_semaphore()
    for other in range(total):
        @pl.when(me != other)
        def _():
            pl.semaphore_signal(
                barrier, inc=1, device_id=(region, other // gy_count, other % gy_count), device_id_type=MESH
            )
    own_rows = pl.ds(OFF, ny)
    own_labels = pl.ds(LH, ny)
    copies = [
        pltpu.make_async_copy(residual, R.at[pl.ds(DEPTH, nz), own_rows], local_sem.at[0]),
        pltpu.make_async_copy(labels, LAB.at[pl.ds(4, nz), own_labels], local_sem.at[1]),
        pltpu.make_async_copy(boundary, BND.at[pl.ds(4, nz), own_labels], local_sem.at[2]),
        pltpu.make_async_copy(iterate, X, local_sem.at[3]),
    ]
    for copy in copies:
        copy.start()
    pl.semaphore_wait(barrier, total - 1)

    steps = (1, -1, 2, -2)

    def target_ok(step):
        return gz + step < gz_count if step > 0 else gz + step >= 0

    def source_ok(step):
        return gz - step >= 0 if step > 0 else gz - step < gz_count

    res_planes = {1: (0, 2, 1), -1: (0, 2, 5), 2: (1, 1, 0), -2: (0, 1, 7)}
    lab_planes = {1: 2, -1: 6, 2: 0, -2: 8}

    def bulk(kind, index, step):
        slot = kind * 4 + index
        if kind == 2:
            first, count, put = res_planes[step]
            src = residual.at[pl.ds(first, count)]
            dst = R.at[pl.ds(put, count), own_rows]
        else:
            src = (labels, boundary)[kind]
            dst = (LAB, BND)[kind].at[pl.ds(lab_planes[step], 2), own_labels]
        return pltpu.make_async_remote_copy(
            src_ref=src, dst_ref=dst, send_sem=bulk_send.at[slot], recv_sem=bulk_recv.at[slot],
            device_id=(region, gz + step, gy), device_id_type=MESH,
        )

    for kind in (0, 1, 2):
        for index, step in enumerate(steps):
            @pl.when(target_ok(step))
            def _():
                bulk(kind, index, step).start()

    def strip(kind, group, side):
        slot = (kind * 5 + group) * 2 + side
        if kind == 2:
            if group == 0:
                put, count = DEPTH, nz
            else:
                _, count, put = res_planes[steps[group - 1]]
            from_row = OFF + ny - YH if side == 0 else OFF
            to_row = OFF - YH if side == 0 else OFF + ny
            size, ref = YH, R
        else:
            put, count = (4, 2) if group == 0 else (lab_planes[steps[group - 1]], 2)
            from_row = ny if side == 0 else LH
            to_row = 0 if side == 0 else LH + ny
            size, ref = LH, (LAB, BND)[kind]
        return pltpu.make_async_remote_copy(
            src_ref=ref.at[pl.ds(put, count), pl.ds(from_row, size)],
            dst_ref=ref.at[pl.ds(put, count), pl.ds(to_row, size)],
            send_sem=strip_send.at[slot], recv_sem=strip_recv.at[slot],
            device_id=(region, gz, gy + (1 if side == 0 else -1)), device_id_type=MESH,
        )

    has_up = gy + 1 < gy_count
    has_down = gy >= 1

    def start_strips(kind, group):
        for side, sends in ((0, has_up), (1, has_down)):
            @pl.when(sends)
            def _():
                strip(kind, group, side).start()

    def finish_strips(kind, group):
        for side, sends, gets in ((0, has_up, has_down), (1, has_down, has_up)):
            @pl.when(gets)
            def _():
                strip(kind, group, side).wait_recv()

            @pl.when(sends)
            def _():
                strip(kind, group, side).wait_send()

    zero_row = jnp.zeros((m, nx), F32)

    def zero_plane(ref, plane):
        def body(j, carry):
            ref[plane, j] = zero_row
            return carry
        lax.fori_loop(0, ny + 2 * OFF, body, 0)

    for index, step in enumerate(steps):
        _, count, put = res_planes[step]

        @pl.when(jnp.logical_not(source_ok(step)))
        def _():
            for plane in range(put, put + count):
                zero_plane(R, plane)
    for plane in range(8):
        for j in list(range(OFF)) + list(range(OFF + ny, 2 * OFF + ny)):
            D[plane, j] = zero_row

    for copy in copies:
        copy.wait()
    for kind in (0, 1, 2):
        start_strips(kind, 0)
    for index, step in enumerate(steps):
        @pl.when(source_ok(step))
        def _():
            for kind in (0, 1):
                bulk(kind, index, step).wait_recv()
                start_strips(kind, 1 + index)
    for kind in (0, 1):
        finish_strips(kind, 0)
    for index, step in enumerate(steps):
        @pl.when(source_ok(step))
        def _():
            for kind in (0, 1):
                finish_strips(kind, 1 + index)

    cell_row = lax.broadcasted_iota(jnp.int32, (ny + 2 * LH, nx), 0)
    cell_col = lax.broadcasted_iota(jnp.int32, (ny + 2 * LH, nx), 1)
    low_row = jnp.where(has_down, 0, LH)
    high_row = jnp.where(has_up, ny + 2 * LH, ny + LH)
    first_plane = 4 - 2 * jnp.minimum(gz, 2)
    last_plane = 6 + 2 * jnp.minimum(gz_count - 1 - gz, 2)

    def coef_body(f, carry):
        there = (cell_row >= jnp.where((f >= first_plane) & (f < last_plane), low_row, ny + 2 * LH)) & (cell_row < high_row)
        coef = jnp.exp(LAB[f].astype(F32) * (contrast_log / (NCLASS - 1)))
        COEF[f] = jnp.where(there, coef, 0.0)
        INNER[f] = jnp.where(there, (1 - BND[f]).astype(F32), 0.0)
        return carry

    lax.fori_loop(0, 10, coef_body, 0)
    rows_cell = ny + 2 * LH

    def field_body(e, carry):
        coef = COEF[e + 1]
        inner = INNER[e + 1]
        diagonal = jnp.zeros_like(coef)
        beside = (
            (WZU, lambda ref: ref[e + 2]),
            (WZD, lambda ref: ref[e]),
            (WYU, lambda ref: pltpu.roll(ref[e + 1], rows_cell - 1, 0)),
            (WYD, lambda ref: pltpu.roll(ref[e + 1], 1, 0)),
            (WXR, lambda ref: jnp.where(cell_col == nx - 1, 0.0, pltpu.roll(ref[e + 1], nx - 1, 1))),
            (WXL, lambda ref: jnp.where(cell_col == 0, 0.0, pltpu.roll(ref[e + 1], 1, 1))),
        )
        for weight, of in beside:
            near = of(COEF)
            face = jnp.where(near > 0.0, 2.0 * coef * near / (coef + near), coef)
            diagonal = diagonal + face
            weight[e] = inner * face * of(INNER)
        diagonal = inner * diagonal + (1.0 - inner)
        DIAG[e] = diagonal
        INV[e] = 1.0 / diagonal
        return carry

    lax.fori_loop(0, 8, field_body, 0)

    def over_rows(first, count, unroll, row):
        def body(i, carry):
            for k in range(unroll):
                row(first + i * unroll + k)
            return carry
        lax.fori_loop(0, count // unroll, body, 0)

    def cell(ref, e, j):
        return ref[e, pl.ds(j + SHIFT, 1), :]

    def scale(planes):
        for e in planes:
            def row(j):
                D[e, j] = cell(INV, e, j) * R[e, j]
            over_rows(start, rows_window, GROUP, row)

    def residual_planes(indices):
        for index in indices:
            @pl.when(source_ok(steps[index]))
            def _():
                bulk(2, index, steps[index]).wait_recv()
                start_strips(2, 1 + index)
        for index in indices:
            @pl.when(source_ok(steps[index]))
            def _():
                finish_strips(2, 1 + index)

    finish_strips(2, 0)
    scale(range(DEPTH, DEPTH + nz))
    residual_planes((0, 1))
    scale((1, 2, 5, 6))

    lane = lax.broadcasted_iota(jnp.int32, (m, 128), 1)
    sub = lax.broadcasted_iota(jnp.int32, (m, 128), 0)

    def place(block, at, to):
        kept = jnp.where((lane >= at) & (lane < at + m), block, 0.0)
        shift = (to - at) % 128
        return pltpu.roll(kept, shift, 1) if shift else kept

    def square(block, at):
        shift = (-at) % 128
        return (pltpu.roll(block, shift, 1) if shift else block)[:, :m]

    def weights(mat_t):
        high = mat_t.astype(BF16).astype(F32)
        rest = mat_t - high
        low = rest.astype(BF16).astype(F32)
        pieces = (high, high, low, high, low, rest - low)
        for i, piece in enumerate(pieces):
            wbuf[:, i * m : (i + 1) * m] = piece
        return wbuf[:, 0 : len(pieces) * m].astype(BF16)

    def mix(left, value):
        high, low = split(value)
        third = (value - high.astype(F32) - low.astype(F32)).astype(BF16)
        pieces = [high, low, high, third, low, high]
        return jnp.dot(left, jnp.concatenate(pieces, axis=0), preferred_element_type=F32)

    own_planes = tuple(range(DEPTH, DEPTH + nz))
    side = GROUP * m

    def gram(pair):
        acc[...] = jnp.zeros_like(acc)
        for e in own_planes:
            def gram_rows(i, carry):
                left, right = pair(e, OFF + i * GROUP)
                left_hi, left_lo = split(left.reshape(side, nx))
                right_hi, right_lo = split(right.reshape(side, nx))
                acc[:, 0:side] += dot_nt(left_hi, right_hi) + (dot_nt(left_hi, right_lo) + dot_nt(left_lo, right_hi))
                return carry
            lax.fori_loop(0, ny // GROUP, gram_rows, 0)
        block = place(acc[0:m, :], 0, 0)
        for i in range(1, GROUP):
            block = block + place(acc[i * m : (i + 1) * m, :], i * m, 0)
        return block

    def residual_pair(e, j):
        res = R[e, pl.ds(j, GROUP)]
        inverse = jnp.stack([jnp.broadcast_to(cell(INV, e, j + k), (m, nx)) for k in range(GROUP)])
        return res, inverse * res

    def direction_pair(e, j):
        return D[e, pl.ds(j, GROUP)], IM[e - 1, pl.ds(j, GROUP)]

    def gram_send_copy(turn, other):
        return pltpu.make_async_remote_copy(
            src_ref=gsend.at[turn], dst_ref=gslots.at[turn, me],
            send_sem=gram_send.at[turn, other], recv_sem=gram_recv.at[turn, me],
            device_id=(region, other // gy_count, other % gy_count), device_id_type=MESH,
        )

    def gram_arrival(turn, other):
        return pltpu.make_async_remote_copy(
            src_ref=gsend.at[turn], dst_ref=gslots.at[turn, other],
            send_sem=gram_send.at[turn, other], recv_sem=gram_recv.at[turn, other],
            device_id=(region, other // gy_count, other % gy_count), device_id_type=MESH,
        )

    def reduce_start(turn, block):
        gsend[turn] = block
        gslots[turn, me] = block
        for other in range(total):
            @pl.when(me != other)
            def _():
                gram_send_copy(turn, other).start()

    def reduce_finish(turn):
        for other in range(total):
            @pl.when(me != other)
            def _():
                gram_arrival(turn, other).wait_recv()
        summed = gslots[turn, 0]
        for other in range(1, total):
            summed = summed + gslots[turn, other]
        for other in range(total):
            @pl.when(me != other)
            def _():
                gram_send_copy(turn, other).wait_send()
        return summed

    def images(planes):
        for e in planes:
            def row(j):
                center = D[e, j]
                coupled = cell(WZU, e, j) * D[e + 1, j] + cell(WZD, e, j) * D[e - 1, j]
                coupled = coupled + cell(WYU, e, j) * D[e, j + 1] + cell(WYD, e, j) * D[e, j - 1]
                coupled = coupled + cell(WXR, e, j) * pltpu.roll(center, nx - 1, 1)
                coupled = coupled + cell(WXL, e, j) * pltpu.roll(center, 1, 1)
                IM[e - 1, j] = cell(DIAG, e, j) * center - coupled
            over_rows(start, rows_window, GROUP, row)

    def residuals(planes, w_step):
        for e in planes:
            def row(j):
                R[e, j] = R[e, j] - mix(w_step, IM[e - 1, j])
            over_rows(start, rows_window, GROUP, row)

    out_it = pltpu.make_async_copy(X, iterate_out, out_sem.at[0])
    out_res = pltpu.make_async_copy(R.at[pl.ds(DEPTH, nz), own_rows], residual_out, out_sem.at[1])
    summed_rho = None
    for it in range(ITERS):
        last = it + 1 == ITERS
        ghosts = [e for e in range(1 + it, 7 - it) if e not in own_planes]
        images(own_planes)
        block = gram(direction_pair)
        if it == 0:
            block = block + pltpu.roll(gram(residual_pair), m, 1)
        reduce_start(2 * it, block)
        if it == 0:
            residual_planes((2, 3))
            scale((0, 7))
        images(ghosts)
        grams = reduce_finish(2 * it)
        if it == 0:
            summed_rho = square(grams, m)
        wbuf[...] = jnp.zeros_like(wbuf)
        wbuf[:, 0:m] = square(grams, 0)
        wbuf[:, m : 2 * m] = summed_rho
        step = square(eliminate(wbuf[...]), m)
        identity = jnp.where(lane == sub, 1.0, 0.0).astype(F32)[:, :m]
        w_step = weights(exact_nt(identity, step))
        residuals(own_planes, w_step)
        if last:
            out_res.start()
        else:
            reduce_start(2 * it + 1, gram(residual_pair))
            residuals(ghosts, w_step)
        for e in own_planes:
            def row(j):
                X[e - DEPTH, j] = X[e - DEPTH, j] + mix(w_step, D[e, j + OFF])
            over_rows(0, ny, GROUP, row)
        if not last:
            wbuf[...] = jnp.where(lane - m == sub, 1.0, 0.0)
            wbuf[:, 0:m] = summed_rho
            inverse_rho = square(eliminate(wbuf[...]), m)
            next_rho = square(reduce_finish(2 * it + 1), 0)
            w_momentum = weights(exact_nt(next_rho, inverse_rho))
            summed_rho = next_rho
            for e in list(own_planes) + ghosts:
                def row(j):
                    D[e, j] = cell(INV, e, j) * R[e, j] + mix(w_momentum, D[e, j])
                over_rows(start, rows_window, GROUP, row)

    out_it.start()
    for kind in (0, 1, 2):
        for index, step in enumerate(steps):
            @pl.when(target_ok(step))
            def _():
                bulk(kind, index, step).wait_send()
    out_it.wait()
    out_res.wait()


def solution(mesh):
    gz_count, gy_count = mesh.shape["gz"], mesh.shape["gy"]
    total = gz_count * gy_count

    def on_device(iterate, residual, labels, boundary):
        m, nz, ny, nx = iterate.shape
        sizes = (gz_count, gy_count, m, nz, ny, nx)
        moved = lambda a: jnp.transpose(a, (1, 2, 0, 3))
        rows, cells = ny + 2 * OFF, ny + 2 * LH
        vmem = lambda *shape: pltpu.VMEM(shape, F32)
        any_spec = pl.BlockSpec(memory_space=pl.ANY)
        shape = jax.ShapeDtypeStruct((nz, ny, m, nx), F32)
        side = GROUP * m
        out = pl.pallas_call(
            functools.partial(kernel, sizes),
            out_shape=(shape, shape),
            in_specs=[any_spec] * 4,
            out_specs=(any_spec, any_spec),
            scratch_shapes=[
                vmem(nz, ny, m, nx), vmem(8, rows, m, nx), vmem(8, rows, m, nx), vmem(6, rows, m, nx),
                pltpu.VMEM((10, cells, nx), jnp.int32), pltpu.VMEM((10, cells, nx), jnp.int32),
                vmem(10, cells, nx), vmem(10, cells, nx),
                *[vmem(8, cells, nx) for _ in range(8)],
                vmem(side, 128), vmem(REDUCES, m, 128), vmem(REDUCES, total, m, 128), vmem(m, 128),
                pltpu.SemaphoreType.DMA((4,)),
                pltpu.SemaphoreType.DMA((12,)), pltpu.SemaphoreType.DMA((12,)),
                pltpu.SemaphoreType.DMA((30,)), pltpu.SemaphoreType.DMA((30,)),
                pltpu.SemaphoreType.DMA((REDUCES, total)), pltpu.SemaphoreType.DMA((REDUCES, total)),
                pltpu.SemaphoreType.DMA((2,)),
            ],
            compiler_params=pltpu.CompilerParams(
                collective_id=0, has_side_effects=True, vmem_limit_bytes=60 * 1024 * 1024
            ),
        )(moved(iterate), moved(residual), labels, boundary)
        back = lambda a: jnp.transpose(a, (2, 0, 1, 3))
        return back(out[0]), back(out[1])

    placed = P(None, ("regions", "gz"), "gy", None)
    cell_placed = P(("regions", "gz"), "gy", None)
    return jax.shard_map(
        on_device,
        mesh=mesh,
        in_specs=(placed, placed, cell_placed, cell_placed),
        out_specs=(placed, placed),
        check_vma=False,
    )
```

```python
import functools
import math

import jax
import jax.numpy as jnp
from jax import lax
from jax.experimental import pallas as pl
from jax.experimental.pallas import tpu as pltpu
from jax.sharding import PartitionSpec as P

NCLASS = 8
ITERS = 3
DEPTH = ITERS
YH = 4
OFF = YH + 1
LH = 8
SHIFT = LH - OFF
GROUP = 4
GRAM_GROUPS = 4
WIDE = 17
REDUCES = 2 * ITERS - 1

contrast_log = 4.0 * math.log(10.0)
MESH = pl.DeviceIdType.MESH
F32 = jnp.float32
BF16 = jnp.bfloat16


def split(value):
    high = value.astype(BF16)
    return high, (value - high.astype(F32)).astype(BF16)


def dot_nt(left, right):
    return lax.dot_general(left, right, (((1,), (1,)), ((), ())), preferred_element_type=F32)


def exact(left, right, contract):
    parts = []
    for value in (left, right):
        first, rest = split(value)
        third = (value - first.astype(F32) - rest.astype(F32)).astype(BF16)
        parts.append((first, rest, third))
    result = None
    for i, j in ((2, 0), (1, 1), (0, 2), (1, 0), (0, 1), (0, 0)):
        term = lax.dot_general(parts[0][i], parts[1][j], (contract, ((), ())), preferred_element_type=F32)
        result = term if result is None else result + term
    return result


def exact_nt(left, right):
    return exact(left, right, ((1,), (1,)))


def exact_nn(left, right):
    return exact(left, right, ((1,), (0,)))


def eliminate(matrix):
    m = matrix.shape[0]
    row_id = lax.broadcasted_iota(jnp.int32, matrix.shape, 0)
    for k in range(m):
        pivot_row = matrix[k : k + 1, :] / matrix[k : k + 1, k : k + 1]
        matrix = jnp.where(row_id == k, pivot_row, matrix - matrix[:, k : k + 1] * pivot_row)
    return matrix


def kernel(
    sizes,
    iterate, residual, labels, boundary, iterate_out, residual_out,
    X, R, D, IM, LAB, BND, COEF, INNER, INV, DIAG, WZU, WZD, WYU, WYD, WXR, WXL,
    acc, gsend, gslots, wbuf,
    local_sem, bulk_send, bulk_recv, strip_send, strip_recv, gram_send, gram_recv, out_sem,
):
    gz_count, gy_count, m, nz, ny, nx = sizes
    total = gz_count * gy_count
    region = lax.axis_index("regions")
    gz = lax.axis_index("gz")
    gy = lax.axis_index("gy")
    me = gz * gy_count + gy
    rows_window = ny + YH if gy_count == 2 else ny + 2 * YH
    start = OFF - YH * jnp.minimum(gy, 1) if gy_count == 2 else OFF - YH

    barrier = pltpu.get_barrier_semaphore()
    for other in range(total):
        @pl.when(me != other)
        def _():
            pl.semaphore_signal(
                barrier, inc=1, device_id=(region, other // gy_count, other % gy_count), device_id_type=MESH
            )
    own_rows = pl.ds(OFF, ny)
    own_labels = pl.ds(LH, ny)
    copies = [
        pltpu.make_async_copy(residual, R.at[pl.ds(DEPTH, nz), own_rows], local_sem.at[0]),
        pltpu.make_async_copy(labels, LAB.at[pl.ds(4, nz), own_labels], local_sem.at[1]),
        pltpu.make_async_copy(boundary, BND.at[pl.ds(4, nz), own_labels], local_sem.at[2]),
        pltpu.make_async_copy(iterate, X, local_sem.at[3]),
    ]
    for copy in copies:
        copy.start()
    pl.semaphore_wait(barrier, total - 1)

    steps = (1, -1, 2, -2)

    def target_ok(step):
        return gz + step < gz_count if step > 0 else gz + step >= 0

    def source_ok(step):
        return gz - step >= 0 if step > 0 else gz - step < gz_count

    res_planes = {1: (0, 2, 1), -1: (0, 2, 5), 2: (1, 1, 0), -2: (0, 1, 7)}
    lab_planes = {1: 2, -1: 6, 2: 0, -2: 8}

    def bulk(kind, index, step):
        slot = kind * 4 + index
        if kind == 2:
            first, count, put = res_planes[step]
            src = residual.at[pl.ds(first, count)]
            dst = R.at[pl.ds(put, count), own_rows]
        else:
            src = (labels, boundary)[kind]
            dst = (LAB, BND)[kind].at[pl.ds(lab_planes[step], 2), own_labels]
        return pltpu.make_async_remote_copy(
            src_ref=src, dst_ref=dst, send_sem=bulk_send.at[slot], recv_sem=bulk_recv.at[slot],
            device_id=(region, gz + step, gy), device_id_type=MESH,
        )

    for kind in (0, 1, 2):
        for index, step in enumerate(steps):
            @pl.when(target_ok(step))
            def _():
                bulk(kind, index, step).start()

    def strip(kind, group, side):
        slot = (kind * 5 + group) * 2 + side
        if kind == 2:
            if group == 0:
                put, count = DEPTH, nz
            else:
                _, count, put = res_planes[steps[group - 1]]
            from_row = OFF + ny - YH if side == 0 else OFF
            to_row = OFF - YH if side == 0 else OFF + ny
            size, ref = YH, R
        else:
            put, count = (4, 2) if group == 0 else (lab_planes[steps[group - 1]], 2)
            from_row = ny if side == 0 else LH
            to_row = 0 if side == 0 else LH + ny
            size, ref = LH, (LAB, BND)[kind]
        return pltpu.make_async_remote_copy(
            src_ref=ref.at[pl.ds(put, count), pl.ds(from_row, size)],
            dst_ref=ref.at[pl.ds(put, count), pl.ds(to_row, size)],
            send_sem=strip_send.at[slot], recv_sem=strip_recv.at[slot],
            device_id=(region, gz, gy + (1 if side == 0 else -1)), device_id_type=MESH,
        )

    has_up = gy + 1 < gy_count
    has_down = gy >= 1

    def start_strips(kind, group):
        for side, sends in ((0, has_up), (1, has_down)):
            @pl.when(sends)
            def _():
                strip(kind, group, side).start()

    def finish_strips(kind, group):
        for side, sends, gets in ((0, has_up, has_down), (1, has_down, has_up)):
            @pl.when(gets)
            def _():
                strip(kind, group, side).wait_recv()

            @pl.when(sends)
            def _():
                strip(kind, group, side).wait_send()

    zero_row = jnp.zeros((m, nx), F32)

    def zero_plane(ref, plane):
        def body(j, carry):
            ref[plane, j] = zero_row
            return carry
        lax.fori_loop(0, ny + 2 * OFF, body, 0)

    for index, step in enumerate(steps):
        _, count, put = res_planes[step]

        @pl.when(jnp.logical_not(source_ok(step)))
        def _():
            for plane in range(put, put + count):
                zero_plane(R, plane)
    for plane in range(8):
        for j in list(range(OFF)) + list(range(OFF + ny, 2 * OFF + ny)):
            D[plane, j] = zero_row

    for copy in copies:
        copy.wait()
    for kind in (0, 1, 2):
        start_strips(kind, 0)
    for index, step in enumerate(steps):
        @pl.when(source_ok(step))
        def _():
            for kind in (0, 1):
                bulk(kind, index, step).wait_recv()
                start_strips(kind, 1 + index)
    for kind in (0, 1):
        finish_strips(kind, 0)
    for index, step in enumerate(steps):
        @pl.when(source_ok(step))
        def _():
            for kind in (0, 1):
                finish_strips(kind, 1 + index)

    cell_row = lax.broadcasted_iota(jnp.int32, (ny + 2 * LH, nx), 0)
    cell_col = lax.broadcasted_iota(jnp.int32, (ny + 2 * LH, nx), 1)
    low_row = jnp.where(has_down, 0, LH)
    high_row = jnp.where(has_up, ny + 2 * LH, ny + LH)
    first_plane = 4 - 2 * jnp.minimum(gz, 2)
    last_plane = 6 + 2 * jnp.minimum(gz_count - 1 - gz, 2)

    def coef_body(f, carry):
        there = (cell_row >= jnp.where((f >= first_plane) & (f < last_plane), low_row, ny + 2 * LH)) & (cell_row < high_row)
        coef = jnp.exp(LAB[f].astype(F32) * (contrast_log / (NCLASS - 1)))
        COEF[f] = jnp.where(there, coef, 0.0)
        INNER[f] = jnp.where(there, (1 - BND[f]).astype(F32), 0.0)
        return carry

    lax.fori_loop(0, 10, coef_body, 0)
    rows_cell = ny + 2 * LH

    def field_body(e, carry):
        coef = COEF[e + 1]
        inner = INNER[e + 1]
        diagonal = jnp.zeros_like(coef)
        beside = (
            (WZU, lambda ref: ref[e + 2]),
            (WZD, lambda ref: ref[e]),
            (WYU, lambda ref: pltpu.roll(ref[e + 1], rows_cell - 1, 0)),
            (WYD, lambda ref: pltpu.roll(ref[e + 1], 1, 0)),
            (WXR, lambda ref: jnp.where(cell_col == nx - 1, 0.0, pltpu.roll(ref[e + 1], nx - 1, 1))),
            (WXL, lambda ref: jnp.where(cell_col == 0, 0.0, pltpu.roll(ref[e + 1], 1, 1))),
        )
        for weight, of in beside:
            near = of(COEF)
            face = jnp.where(near > 0.0, 2.0 * coef * near / (coef + near), coef)
            diagonal = diagonal + face
            weight[e] = inner * face * of(INNER)
        diagonal = inner * diagonal + (1.0 - inner)
        DIAG[e] = diagonal
        INV[e] = 1.0 / diagonal
        return carry

    lax.fori_loop(0, 8, field_body, 0)

    def over_rows(first, count, unroll, row):
        def body(i, carry):
            for k in range(unroll):
                row(first + i * unroll + k)
            return carry
        lax.fori_loop(0, count // unroll, body, 0)
        for k in range(count // unroll * unroll, count):
            row(first + k)

    def cell(ref, e, j):
        return ref[e, pl.ds(j + SHIFT, 1), :]

    def scale(planes):
        for e in planes:
            def row(j):
                D[e, j] = cell(INV, e, j) * R[e, j]
            over_rows(start, rows_window, GROUP, row)

    def residual_planes(indices):
        for index in indices:
            @pl.when(source_ok(steps[index]))
            def _():
                bulk(2, index, steps[index]).wait_recv()
                start_strips(2, 1 + index)
        for index in indices:
            @pl.when(source_ok(steps[index]))
            def _():
                finish_strips(2, 1 + index)

    finish_strips(2, 0)
    scale(range(DEPTH, DEPTH + nz))
    residual_planes((0, 1))
    scale((1, 2, 5, 6))

    lane = lax.broadcasted_iota(jnp.int32, (m, 128), 1)
    sub = lax.broadcasted_iota(jnp.int32, (m, 128), 0)

    def place(block, at, to):
        kept = jnp.where((lane >= at) & (lane < at + m), block, 0.0)
        shift = (to - at) % 128
        return pltpu.roll(kept, shift, 1) if shift else kept

    def square(block, at):
        shift = (-at) % 128
        return (pltpu.roll(block, shift, 1) if shift else block)[:, :m]

    def weights(mat_t):
        high = mat_t.astype(BF16).astype(F32)
        rest = mat_t - high
        low = rest.astype(BF16).astype(F32)
        pieces = (high, high, low, high, low, rest - low)
        for i, piece in enumerate(pieces):
            wbuf[:, i * m : (i + 1) * m] = piece
        return wbuf[:, 0 : len(pieces) * m].astype(BF16)

    def mix(left, value):
        high, low = split(value)
        third = (value - high.astype(F32) - low.astype(F32)).astype(BF16)
        pieces = [high, low, high, third, low, high]
        return jnp.dot(left, jnp.concatenate(pieces, axis=0), preferred_element_type=F32)

    own_planes = tuple(range(DEPTH, DEPTH + nz))
    side = GROUP * m

    def gram(pair):
        acc[...] = jnp.zeros_like(acc)
        for e in own_planes:
            def gram_rows(i, carry):
                part = None
                for k in range(GRAM_GROUPS):
                    left, right = pair(e, OFF + (i * GRAM_GROUPS + k) * GROUP)
                    left_hi, left_lo = split(left.reshape(side, nx))
                    right_hi, right_lo = split(right.reshape(side, nx))
                    term = dot_nt(left_hi, right_hi) + (dot_nt(left_hi, right_lo) + dot_nt(left_lo, right_hi))
                    part = term if part is None else part + term
                acc[:, 0:side] += part
                return carry
            lax.fori_loop(0, ny // (GROUP * GRAM_GROUPS), gram_rows, 0)
        block = place(acc[0:m, :], 0, 0)
        for i in range(1, GROUP):
            block = block + place(acc[i * m : (i + 1) * m, :], i * m, 0)
        return block

    def residual_pair(e, j):
        res = R[e, pl.ds(j, GROUP)]
        inverse = jnp.stack([jnp.broadcast_to(cell(INV, e, j + k), (m, nx)) for k in range(GROUP)])
        return res, inverse * res

    def direction_pair(e, j):
        return D[e, pl.ds(j, GROUP)], IM[e - 1, pl.ds(j, GROUP)]

    def gram_send_copy(turn, other):
        return pltpu.make_async_remote_copy(
            src_ref=gsend.at[turn], dst_ref=gslots.at[turn, me],
            send_sem=gram_send.at[turn, other], recv_sem=gram_recv.at[turn, me],
            device_id=(region, other // gy_count, other % gy_count), device_id_type=MESH,
        )

    def gram_arrival(turn, other):
        return pltpu.make_async_remote_copy(
            src_ref=gsend.at[turn], dst_ref=gslots.at[turn, other],
            send_sem=gram_send.at[turn, other], recv_sem=gram_recv.at[turn, other],
            device_id=(region, other // gy_count, other % gy_count), device_id_type=MESH,
        )

    def reduce_start(turn, block):
        gsend[turn] = block
        gslots[turn, me] = block
        for other in range(total):
            @pl.when(me != other)
            def _():
                gram_send_copy(turn, other).start()

    def reduce_finish(turn):
        for other in range(total):
            @pl.when(me != other)
            def _():
                gram_arrival(turn, other).wait_recv()
        summed = gslots[turn, 0]
        for other in range(1, total):
            summed = summed + gslots[turn, other]
        for other in range(total):
            @pl.when(me != other)
            def _():
                gram_send_copy(turn, other).wait_send()
        return summed

    def images(planes):
        for e in planes:
            def row(j):
                center = D[e, j]
                coupled = cell(WZU, e, j) * D[e + 1, j] + cell(WZD, e, j) * D[e - 1, j]
                coupled = coupled + cell(WYU, e, j) * D[e, j + 1] + cell(WYD, e, j) * D[e, j - 1]
                coupled = coupled + cell(WXR, e, j) * pltpu.roll(center, nx - 1, 1)
                coupled = coupled + cell(WXL, e, j) * pltpu.roll(center, 1, 1)
                IM[e - 1, j] = cell(DIAG, e, j) * center - coupled
            over_rows(start, rows_window, WIDE, row)

    def residuals(planes, w_step):
        for e in planes:
            def row(j):
                R[e, j] = R[e, j] - mix(w_step, IM[e - 1, j])
            over_rows(start, rows_window, WIDE, row)

    out_it = pltpu.make_async_copy(X, iterate_out, out_sem.at[0])
    out_res = pltpu.make_async_copy(R.at[pl.ds(DEPTH, nz), own_rows], residual_out, out_sem.at[1])
    summed_rho = None
    for it in range(ITERS):
        last = it + 1 == ITERS
        ghosts = [e for e in range(1 + it, 7 - it) if e not in own_planes]
        images(own_planes)
        block = gram(direction_pair)
        if it == 0:
            block = block + pltpu.roll(gram(residual_pair), m, 1)
        reduce_start(2 * it, block)
        if it == 0:
            residual_planes((2, 3))
            scale((0, 7))
        images(ghosts)
        grams = reduce_finish(2 * it)
        if it == 0:
            summed_rho = square(grams, m)
        wbuf[...] = jnp.zeros_like(wbuf)
        wbuf[:, 0:m] = square(grams, 0)
        wbuf[:, m : 2 * m] = summed_rho
        step = square(eliminate(wbuf[...]), m)
        identity = jnp.where(lane == sub, 1.0, 0.0).astype(F32)[:, :m]
        w_step = weights(exact_nt(identity, step))
        residuals(own_planes, w_step)
        if last:
            out_res.start()
        else:
            reduce_start(2 * it + 1, gram(residual_pair))
            residuals(ghosts, w_step)
        for e in own_planes:
            def row(j):
                X[e - DEPTH, j] = X[e - DEPTH, j] + mix(w_step, D[e, j + OFF])
            over_rows(0, ny, 4 * GROUP, row)
        if not last:
            wbuf[...] = jnp.where(lane - m == sub, 1.0, 0.0)
            wbuf[:, 0:m] = summed_rho
            inverse_rho = square(eliminate(wbuf[...]), m)
            next_rho = square(reduce_finish(2 * it + 1), 0)
            w_momentum = weights(exact_nt(next_rho, inverse_rho))
            summed_rho = next_rho
            for e in list(own_planes) + ghosts:
                def row(j):
                    D[e, j] = cell(INV, e, j) * R[e, j] + mix(w_momentum, D[e, j])
                over_rows(start, rows_window, WIDE, row)

    out_it.start()
    for kind in (0, 1, 2):
        for index, step in enumerate(steps):
            @pl.when(target_ok(step))
            def _():
                bulk(kind, index, step).wait_send()
    out_it.wait()
    out_res.wait()


def solution(mesh):
    gz_count, gy_count = mesh.shape["gz"], mesh.shape["gy"]
    total = gz_count * gy_count

    def on_device(iterate, residual, labels, boundary):
        m, nz, ny, nx = iterate.shape
        sizes = (gz_count, gy_count, m, nz, ny, nx)
        moved = lambda a: jnp.transpose(a, (1, 2, 0, 3))
        rows, cells = ny + 2 * OFF, ny + 2 * LH
        vmem = lambda *shape: pltpu.VMEM(shape, F32)
        any_spec = pl.BlockSpec(memory_space=pl.ANY)
        shape = jax.ShapeDtypeStruct((nz, ny, m, nx), F32)
        side = GROUP * m
        out = pl.pallas_call(
            functools.partial(kernel, sizes),
            out_shape=(shape, shape),
            in_specs=[any_spec] * 4,
            out_specs=(any_spec, any_spec),
            scratch_shapes=[
                vmem(nz, ny, m, nx), vmem(8, rows, m, nx), vmem(8, rows, m, nx), vmem(6, rows, m, nx),
                pltpu.VMEM((10, cells, nx), jnp.int32), pltpu.VMEM((10, cells, nx), jnp.int32),
                vmem(10, cells, nx), vmem(10, cells, nx),
                *[vmem(8, cells, nx) for _ in range(8)],
                vmem(side, 128), vmem(REDUCES, m, 128), vmem(REDUCES, total, m, 128), vmem(m, 128),
                pltpu.SemaphoreType.DMA((4,)),
                pltpu.SemaphoreType.DMA((12,)), pltpu.SemaphoreType.DMA((12,)),
                pltpu.SemaphoreType.DMA((30,)), pltpu.SemaphoreType.DMA((30,)),
                pltpu.SemaphoreType.DMA((REDUCES, total)), pltpu.SemaphoreType.DMA((REDUCES, total)),
                pltpu.SemaphoreType.DMA((2,)),
            ],
            compiler_params=pltpu.CompilerParams(
                collective_id=0, has_side_effects=True, vmem_limit_bytes=60 * 1024 * 1024
            ),
        )(moved(iterate), moved(residual), labels, boundary)
        back = lambda a: jnp.transpose(a, (2, 0, 1, 3))
        return back(out[0]), back(out[1])

    placed = P(None, ("regions", "gz"), "gy", None)
    cell_placed = P(("regions", "gz"), "gy", None)
    return jax.shard_map(
        on_device,
        mesh=mesh,
        in_specs=(placed, placed, cell_placed, cell_placed),
        out_specs=(placed, placed),
        check_vma=False,
    )
```
